256 devices in a mesh: row: 32 (over x_lo, z, core), col: 8 (over y, x_hi).
Axes of the slice: x: 4 (x_hi: 2, x_lo: 2; x = x_hi * 2 + x_lo), y: 4, z: 8, core: 2. Of those that a mesh axis runs over, the one named last changes fastest.
Arguments:
- trail_adjoint: float32 [32, 512, 8, 2048], P('row', None, 'col'), may hold values from -2.8 to 2.8, as said below
- panel_one: float32 [16384, 512], P(('row', 'col')), may hold values from -0.046875 to 0.046875
- panel_two: float32 [16384, 512], P(('row', 'col')), may hold values from -0.046875 to 0.046875
- upstream_one: float32 [16384, 512], P(('row', 'col')), may hold values from -6 to 6
- upstream_two: float32 [16384, 512], P(('row', 'col')), may hold values from -6 to 6
- pivot_one: float32 [512, 512], replicated, may hold values from -1 to 2, as said below
- pivot_two: float32 [512, 512], replicated, may hold values from -1 to 2, as said below
- link_block: float32 [512, 512], replicated, may hold values from -0.25 to 0.25
- pivot_adjoint: float32 [2, 512, 512], replicated, may hold values from -6 to 6
Outputs:
- strip_grad_one: float32 [16384, 512], P(('row', 'col'))
- strip_grad_two: float32 [16384, 512], P(('row', 'col'))
- block_grads: float32 [3, 512, 512], replicated
The draws below stay inside these ranges and needn't reach their ends.
Inputs may be any that keep to these rules, and one draw needn't show every extreme that they name: trail_adjoint[a, c * 64 + s, c2, a2 * 64 + s2] equals trail_adjoint[a2, c2 * 64 + s2, c, a * 64 + s], so sbar is symmetric. `pivot_one`: lower triangular, diagonal entries between 1 and 2. `pivot_two`: lower triangular, diagonal entries between 1 and 2.
All inputs are finite; a program needn't handle non-finite values.
Results may differ from the reference program's by a relative error of at most 0.000062.
Values sent between devices are 32-bit elements; how exact they have to be, the bound alone decides.
No kernel may reach another device: no remote copies, remote signals or barrier semaphores. Data moves between devices by JAX's collectives and lax.ppermute only.
A program may use at most 128 MiB of HBM per device.

```python
import math
import jax
import jax.numpy as jnp
from jax import lax

PANEL_WIDTH = 512
SLAB_ROWS = 64
GRID_ROWS = 32
GRID_COLS = 8
TRAIL_ROWS = 16384


def lower_factor(base_key):
    diag_key, off_key = jax.random.split(base_key)
    diagonal = jax.random.uniform(diag_key, (PANEL_WIDTH,), jnp.float32, 1.0, 2.0)
    strict_part = jnp.clip(jax.random.normal(off_key, (PANEL_WIDTH, PANEL_WIDTH), jnp.float32), -4.0, 4.0)
    strict_part = strict_part * (0.45 / math.sqrt(PANEL_WIDTH))
    return jnp.tril(strict_part, -1) + jnp.diag(diagonal)


def draw_pivot_one(key, part):
    return lower_factor(jax.random.fold_in(key, 11))


def draw_pivot_two(key, part):
    return lower_factor(jax.random.fold_in(key, 23))


def draw_trail_adjoint(key, part):
    shape_six = (GRID_ROWS, GRID_COLS, SLAB_ROWS, GRID_COLS, GRID_ROWS, SLAB_ROWS)
    raw_values = jnp.clip(jax.random.normal(jax.random.fold_in(key, 37), shape_six, jnp.float32), -4.0, 4.0) * 0.7
    mirrored = 0.5 * (raw_values + jnp.transpose(raw_values, (4, 3, 5, 1, 0, 2)))
    return mirrored.reshape(GRID_ROWS, GRID_COLS * SLAB_ROWS, GRID_COLS, GRID_ROWS * SLAB_ROWS)


def block_scale(rng, dims, cuts, low, high):
    loudness, own = 1.0, jax.random.fold_in(rng, 6)
    for axis_at, blocks in cuts:
        heights = jnp.exp(jax.random.uniform(jax.random.fold_in(own, axis_at), (blocks,), jnp.float32, low / len(cuts), high / len(cuts)))
        loudness = loudness * jnp.repeat(heights, dims[axis_at] // blocks).reshape([-1 if axis == axis_at else 1 for axis in range(len(dims))])
    return loudness


def scatter_about(key, extent, scale, bound, cuts=(), kind=jnp.bfloat16):
    drawn = jax.random.normal(key, extent, jnp.float32) * scale
    if len(cuts) > 0:
        drawn = block_scale(key, extent, cuts, -0.22, 0.18) * drawn
    return jnp.clip(drawn, min=-bound, max=bound).astype(kind)


def setup_inputs(seed: int = 0) -> dict:
    arg_keys = jax.random.split(jax.random.key(seed), 10)
    return {
        "trail_adjoint": draw_trail_adjoint(jax.random.fold_in(arg_keys[9], 71), 0),
        "panel_one": scatter_about(arg_keys[1], (TRAIL_ROWS, PANEL_WIDTH), TRAIL_ROWS ** -0.5, 0.046875, ((0, 256),), jnp.float32),
        "panel_two": scatter_about(arg_keys[2], (TRAIL_ROWS, PANEL_WIDTH), TRAIL_ROWS ** -0.5, 0.046875, ((0, 256),), jnp.float32),
        "upstream_one": scatter_about(arg_keys[3], (TRAIL_ROWS, PANEL_WIDTH), 1.0, 6.0, ((0, 256),), jnp.float32),
        "upstream_two": scatter_about(arg_keys[4], (TRAIL_ROWS, PANEL_WIDTH), 1.0, 6.0, ((0, 256),), jnp.float32),
        "pivot_one": draw_pivot_one(jax.random.fold_in(arg_keys[9], 71), 0),
        "pivot_two": draw_pivot_two(jax.random.fold_in(arg_keys[9], 71), 0),
        "link_block": scatter_about(arg_keys[7], (PANEL_WIDTH, PANEL_WIDTH), PANEL_WIDTH ** -0.5, 0.25, (), jnp.float32),
        "pivot_adjoint": scatter_about(arg_keys[8], (2, PANEL_WIDTH, PANEL_WIDTH), 1.0, 6.0, (), jnp.float32),
    }


def exact_dot(left, right):
    return jnp.dot(left.astype(jnp.float32), right.astype(jnp.float32), precision=lax.Precision.HIGHEST, preferred_element_type=jnp.float32)

def cross_dot(left, right):
    return lax.dot_general(left.astype(jnp.float32), right.astype(jnp.float32), (((0,), (0,)), ((), ())), precision=lax.Precision.HIGHEST, preferred_element_type=jnp.float32)

def lower_inverse(factor):
    identity = jnp.eye(factor.shape[0], dtype=jnp.float32)
    return jax.scipy.linalg.solve_triangular(factor, identity, lower=True)

def chol_grad(factor, cotangent, inverse):
    product = cross_dot(factor, jnp.tril(cotangent))
    halved = jnp.tril(product) - 0.5 * jnp.diag(jnp.diag(product))
    inner = cross_dot(inverse, exact_dot(halved, inverse))
    return 0.5 * (inner + inner.T)

def reference(trail_adjoint, panel_one, panel_two, upstream_one, upstream_two, pivot_one, pivot_two, link_block, pivot_adjoint):
    width = panel_one.shape[1]
    stacked = jnp.concatenate([panel_one, panel_two], axis=1)
    reordered = stacked.reshape(GRID_ROWS, GRID_COLS, SLAB_ROWS, 2 * width)
    reordered = jnp.transpose(reordered, (1, 0, 2, 3)).reshape(GRID_COLS, GRID_ROWS * SLAB_ROWS, 2 * width)

    def outer_block(slab_block):
        return 2.0 * jnp.einsum('pcq,cqk->pk', slab_block, reordered, precision=lax.Precision.HIGHEST)
    carried = lax.map(outer_block, trail_adjoint).reshape(TRAIL_ROWS, 2 * width)
    pressed_one = upstream_one - carried[:, :width]
    pressed_two = upstream_two - carried[:, width:]
    inverse_one = lower_inverse(pivot_one)
    inverse_two = lower_inverse(pivot_two)
    grad_two = exact_dot(pressed_two, inverse_two)
    cross_two = cross_dot(grad_two, panel_two)
    cross_link = cross_dot(grad_two, panel_one)
    grad_one = exact_dot(pressed_one - exact_dot(grad_two, link_block), inverse_one)
    cross_one = cross_dot(grad_one, panel_one)
    pivot_grad_two = chol_grad(pivot_two, pivot_adjoint[1] - cross_two, inverse_two)
    link_grad = -cross_link - 2.0 * exact_dot(pivot_grad_two, link_block)
    link_input = exact_dot(link_grad, inverse_one)
    pivot_grad_one = chol_grad(pivot_one, pivot_adjoint[0] - cross_dot(link_input, link_block) - cross_one, inverse_one)
    return (grad_one, grad_two, jnp.stack([pivot_grad_one, link_input, pivot_grad_two]))
```

```python
import jax
import jax.numpy as jnp
from jax import lax
from jax.experimental import pallas as pl
from jax.experimental.pallas import tpu as pltpu
from jax.sharding import Mesh, PartitionSpec as P

AXES = ("xl", "z", "core", "y", "xh")
ROW = ("xl", "z", "core")
COL = ("y", "xh")
PLANE = ("y", "xh", "xl")
HIGHEST = lax.Precision.HIGHEST
HIGH = lax.Precision.HIGH
SWAP = [(0, 1), (1, 0)]
W = 512
BASE = 16
VMEM_SPEC = pl.BlockSpec(memory_space=pltpu.VMEM)


def dot(left, right, precision=HIGHEST):
    return jnp.dot(left, right, precision=precision, preferred_element_type=jnp.float32)


def cross(left, right, precision=HIGHEST):
    return lax.dot_general(
        left, right, (((0,), (0,)), ((), ())), precision=precision, preferred_element_type=jnp.float32
    )


def iota(shape, dim):
    return lax.broadcasted_iota(jnp.int32, shape, dim)


def inverse_of(f_ref, v_ref):
    b = BASE
    lane = iota((b, W), 1)
    row = iota((b, W), 0)
    diag = jnp.zeros((b, W), jnp.float32)
    for k in range(W // b):
        diag = jnp.where(lane // b == k, f_ref[k * b : (k + 1) * b, :], diag)
    spread = (iota((128, 128), 0) // b == iota((128, 128), 1) // b).astype(jnp.float32)
    columns = []
    for t in range(W // 128):
        part = diag[:, t * 128 : (t + 1) * 128]
        inner = iota((b, 128), 1) % b
        stack = jnp.concatenate([jnp.where(inner == k, part, 0.0) for k in range(b)], axis=0)
        columns.append(dot(stack, spread))
    spread_f = jnp.concatenate(columns, axis=1)
    x = (lane % b == row).astype(jnp.float32)
    for k in range(b):
        f_k = spread_f[k * b : (k + 1) * b, :]
        x_k = x[k : k + 1, :] / f_k[k : k + 1, :]
        x = jnp.where(row == k, x_k, jnp.where(row > k, x - f_k * x_k, x))
    v_ref[...] = jnp.zeros((W, W), jnp.float32)
    r, c = iota((128, 128), 0), iota((128, 128), 1)
    for t in range(W // 128):
        s = slice(t * 128, (t + 1) * 128)
        part = jnp.concatenate([x[:, s]] * (128 // b), axis=0)
        v = jnp.where(r // b == c // b, part, 0.0)
        f = f_ref[s, s]
        size = b
        while size < 128:
            mask = (r // (2 * size) == c // (2 * size)) & (r // size > c // size)
            v = v - dot(v, dot(jnp.where(mask, f, 0.0), v))
            size *= 2
        v_ref[s, s] = v
    size = 128
    while size < W:
        for t in range(0, W, 2 * size):
            lo, hi = slice(t, t + size), slice(t + size, t + 2 * size)
            v_ref[hi, lo] = -dot(v_ref[hi, hi], dot(f_ref[hi, lo], v_ref[lo, lo]))
        size *= 2


def inverse_kernel(f1_ref, f2_ref, v1_ref, v2_ref):
    inverse_of(f1_ref, v1_ref)
    inverse_of(f2_ref, v2_ref)


def inverses(f1, f2):
    shape = jax.ShapeDtypeStruct((W, W), jnp.float32)
    return pl.pallas_call(
        inverse_kernel,
        out_shape=(shape, shape),
        in_specs=[VMEM_SPEC] * 2,
        out_specs=(VMEM_SPEC,) * 2,
        compiler_params=pltpu.CompilerParams(vmem_limit_bytes=32 << 20),
        cost_estimate=pl.CostEstimate(flops=10**10, bytes_accessed=4 << 20, transcendentals=0),
        name="inverses",
    )(f1, f2)


def split(x):
    hi = x.astype(jnp.bfloat16)
    return hi, (x - hi.astype(jnp.float32)).astype(jnp.bfloat16)


def dot_split(left, right, dims=(((1,), (0,)), ((), ()))):
    (a, b), (c, d) = left, right

    def one(x, y):
        return lax.dot_general(x, y, dims, preferred_element_type=jnp.float32)

    return one(a, c) + (one(b, c) + one(a, d))


def dot3(left, right):
    return dot_split(split(left), split(right))


def cross3(left, right):
    return dot_split(split(left), split(right), (((0,), (0,)), ((), ())))


CHUNKS, CHUNK_ROWS = 16, 136


def sums_kernel(core_ref, s_ref, g_ref, la_ref, u1_ref, u2_ref, l1_ref, l2_ref, p_ref, keep_ref, send_ref):
    step = pl.program_id(0)
    part = dot3(s_ref[...], g_ref[...])

    @pl.when(step == 0)
    def _():
        p_ref[...] = part

    @pl.when(step > 0)
    def _():
        p_ref[...] += part

    @pl.when(step == pl.num_programs(0) - 1)
    def _():
        p_ref[...] = -2.0 * p_ref[...]
        a22 = cross3(p_ref[:, W:], la_ref[:, W:]) + cross3(u2_ref[...], l2_ref[...])
        a21 = cross3(p_ref[:, W:], la_ref[:, :W]) + cross3(u2_ref[...], l1_ref[...])
        a11t = cross3(la_ref[:, :W], p_ref[:, :W]) + cross3(l1_ref[...], u1_ref[...])
        r, c = iota((W, W), 0), iota((W, W), 1)
        mixed = jnp.where(r >= c, a22, a11t)
        diagonal = jnp.sum(jnp.where(r == c, a11t, 0.0), axis=0, keepdims=True)

        def write(ref, x):
            for i in range(CHUNKS):
                for t in range(4):
                    ref[i, t * 32 : (t + 1) * 32, :] = x[i * 32 : (i + 1) * 32, t * 128 : (t + 1) * 128]
            ref[:, 128:, :] = jnp.zeros((CHUNKS, 8, 128), jnp.float32)

        def write_diagonal(ref):
            for t in range(4):
                ref[0, 128 + t : 129 + t, :] = diagonal[:, t * 128 : (t + 1) * 128]

        @pl.when(core_ref[0] == 0)
        def _():
            write(keep_ref, mixed)
            write_diagonal(keep_ref)
            write(send_ref, a21)

        @pl.when(core_ref[0] != 0)
        def _():
            write(keep_ref, a21)
            write(send_ref, mixed)
            write_diagonal(send_ref)


def sums(core, matrix, gathered, block_row, u1, u2, l1, l2):
    step = 512
    half = jax.ShapeDtypeStruct((CHUNKS, CHUNK_ROWS, 128), jnp.float32)
    return pl.pallas_call(
        sums_kernel,
        grid=(matrix.shape[1] // step,),
        out_shape=(jax.ShapeDtypeStruct((W, 2 * W), jnp.float32), half, half),
        in_specs=[
            pl.BlockSpec(memory_space=pltpu.SMEM),
            pl.BlockSpec((W, step), lambda k: (0, k)),
            pl.BlockSpec((step, 2 * W), lambda k: (k, 0)),
        ]
        + [VMEM_SPEC] * 5,
        out_specs=(VMEM_SPEC,) * 3,
        compiler_params=pltpu.CompilerParams(vmem_limit_bytes=48 << 20),
        cost_estimate=pl.CostEstimate(flops=10**10, bytes_accessed=20 << 20, transcendentals=0),
        name="sums",
    )(core, matrix, gathered, block_row, u1, u2, l1, l2)


def chol_grad(f, x, v, r, c):
    product = cross3(f, jnp.where(r >= c, x, 0.0))
    halved = jnp.where(r > c, product, jnp.where(r == c, 0.5 * product, 0.0))
    inner = cross3(v, dot3(halved, v))
    return 0.5 * (inner + inner.T)


def tail_kernel(
    core_ref, half_ref, other_ref, f1_ref, f2_ref, v1_ref, v2_ref, link_ref, adj_ref, out_ref, mixed_ref, a21_ref
):
    def read(ref, source):
        for i in range(CHUNKS):
            for t in range(4):
                ref[i * 32 : (i + 1) * 32, t * 128 : (t + 1) * 128] = source[i, t * 32 : (t + 1) * 32, :]

    first = core_ref[0] == 0

    @pl.when(first)
    def _():
        read(mixed_ref, half_ref)
        read(a21_ref, other_ref)

    @pl.when(jnp.logical_not(first))
    def _():
        read(mixed_ref, other_ref)
        read(a21_ref, half_ref)

    r, c = iota((W, W), 0), iota((W, W), 1)
    rows = jnp.where(first, half_ref[0, 128:, :], other_ref[0, 128:, :])
    diagonal = jnp.concatenate([rows[t : t + 1, :] for t in range(4)], axis=1)
    mixed = mixed_ref[...]
    a22 = jnp.where(r >= c, mixed, 0.0)
    a11 = jnp.where(r > c, mixed.T, jnp.where(r == c, diagonal, 0.0))
    link, v1, v2 = link_ref[...], v1_ref[...], v2_ref[...]
    grad_two = chol_grad(f2_ref[...], adj_ref[1] - cross3(v2, a22), v2, r, c)
    out_ref[2] = grad_two
    cross_link = cross3(v2, a21_ref[...])
    cross_one = cross3(v1, a11 - cross3(link, cross_link))
    link_input = dot3(-cross_link - 2.0 * dot3(grad_two, link), v1)
    out_ref[1] = link_input
    out_ref[0] = chol_grad(f1_ref[...], adj_ref[0] - cross3(link_input, link) - cross_one, v1, r, c)


def tail(core, *operands):
    return pl.pallas_call(
        tail_kernel,
        out_shape=jax.ShapeDtypeStruct((3, W, W), jnp.float32),
        in_specs=[pl.BlockSpec(memory_space=pltpu.SMEM)] + [VMEM_SPEC] * 8,
        out_specs=VMEM_SPEC,
        scratch_shapes=[pltpu.VMEM((W, W), jnp.float32)] * 2,
        compiler_params=pltpu.CompilerParams(vmem_limit_bytes=48 << 20),
        cost_estimate=pl.CostEstimate(flops=10**10, bytes_accessed=14 << 20, transcendentals=0),
        name="tail",
    )(core, *operands)


def reduce_all(keep, send):
    half = keep + lax.ppermute(send, "core", SWAP)
    share = jnp.sum(lax.all_to_all(half, PLANE, 0, 0, tiled=True), axis=0)
    for d in (1, 2, 4):
        share = share + lax.ppermute(share, "z", [(i, i ^ d) for i in range(8)])
    half = lax.all_to_all(jnp.broadcast_to(share, half.shape), PLANE, 0, 0, tiled=True)
    return half, lax.ppermute(half, "core", SWAP)


def local(trail, l1, l2, u1, u2, f1, f2, link, adjoint):
    core = lax.axis_index("core").reshape(1)
    own = jnp.concatenate([l1, l2], axis=1)
    gathered = lax.all_gather(own, ROW, axis=0, tiled=True)
    block_row = lax.all_to_all(jnp.tile(own, (8, 1)), COL, 0, 0, tiled=True)
    matrix = trail.reshape(W, 2048)
    v1, v2 = inverses(f1, f2)
    gathered, block_row, matrix, v1, v2 = lax.optimization_barrier((gathered, block_row, matrix, v1, v2))
    product, keep, send = sums(core, matrix, gathered, block_row, u1, u2, l1, l2)
    half, other = reduce_all(keep, send)
    product, half, other = lax.optimization_barrier((product, half, other))
    mine = lax.all_to_all(product, COL, 0, 0, tiled=True)
    grads = tail(core, half, other, f1, f2, v1, v2, link, adjoint)
    pressed = jnp.sum(mine.reshape(8, 64, 2 * W), axis=0)
    grad_two = dot(u2 + pressed[:, W:], v2)
    grad_one = dot(u1 + pressed[:, :W] - dot(grad_two, link), v1)
    return grad_one, grad_two, grads


def solution(mesh):
    fine = Mesh(mesh.devices.reshape(2, 8, 2, 4, 2), AXES)
    strip = P(ROW + COL, None)
    return jax.shard_map(
        local,
        mesh=fine,
        in_specs=(P(ROW, None, COL, None), strip, strip, strip, strip, P(), P(), P(), P()),
        out_specs=(strip, strip, P()),
        check_vma=False,
    )
```

```python
import jax
import jax.numpy as jnp
from jax import lax
from jax.experimental import pallas as pl
from jax.experimental.pallas import tpu as pltpu
from jax.sharding import Mesh, PartitionSpec as P

AXES = ("xl", "z", "core", "y", "xh")
ROW = ("xl", "z", "core")
COL = ("y", "xh")
PLANE = ("y", "xh", "xl")
HIGHEST = lax.Precision.HIGHEST
HIGH = lax.Precision.HIGH
SWAP = [(0, 1), (1, 0)]
W = 512
BASE = 16
VMEM_SPEC = pl.BlockSpec(memory_space=pltpu.VMEM)
SMEM_SPEC = pl.BlockSpec(memory_space=pltpu.SMEM)


def whole(x):
    return pl.BlockSpec(x.shape, lambda _: (0,) * len(x.shape), pipeline_mode=pl.Buffered(1))


def call(kernel, outs, operands, scratch=(), flops=10**9, name=None):
    return pl.pallas_call(
        kernel,
        grid=(1,),
        out_shape=outs,
        in_specs=[SMEM_SPEC] + [whole(x) for x in operands[1:]],
        out_specs=jax.tree.map(whole, outs),
        scratch_shapes=list(scratch),
        compiler_params=pltpu.CompilerParams(vmem_limit_bytes=62 << 20),
        cost_estimate=pl.CostEstimate(flops=flops, bytes_accessed=16 << 20, transcendentals=0),
        name=name,
    )(*operands)


def floats(*shape):
    return jax.ShapeDtypeStruct(shape, jnp.float32)


def dot(left, right, precision=HIGHEST):
    return jnp.dot(left, right, precision=precision, preferred_element_type=jnp.float32)


def cross(left, right, precision=HIGHEST):
    return lax.dot_general(
        left, right, (((0,), (0,)), ((), ())), precision=precision, preferred_element_type=jnp.float32
    )


def iota(shape, dim):
    return lax.broadcasted_iota(jnp.int32, shape, dim)


def inverse_of(f_ref, v_ref):
    b = BASE
    lane = iota((b, W), 1)
    row = iota((b, W), 0)
    diag = jnp.zeros((b, W), jnp.float32)
    for k in range(W // b):
        diag = jnp.where(lane // b == k, f_ref[k * b : (k + 1) * b, :], diag)
    spread = (iota((128, 128), 0) // b == iota((128, 128), 1) // b).astype(jnp.float32)
    columns = []
    for t in range(W // 128):
        part = diag[:, t * 128 : (t + 1) * 128]
        inner = iota((b, 128), 1) % b
        stack = jnp.concatenate([jnp.where(inner == k, part, 0.0) for k in range(b)], axis=0)
        columns.append(dot(stack, spread))
    spread_f = jnp.concatenate(columns, axis=1)
    x = (lane % b == row).astype(jnp.float32)
    for k in range(b):
        f_k = spread_f[k * b : (k + 1) * b, :]
        x_k = x[k : k + 1, :] / f_k[k : k + 1, :]
        x = jnp.where(row == k, x_k, jnp.where(row > k, x - f_k * x_k, x))
    v_ref[...] = jnp.zeros((W, W), jnp.float32)
    r, c = iota((128, 128), 0), iota((128, 128), 1)
    for t in range(W // 128):
        s = slice(t * 128, (t + 1) * 128)
        part = jnp.concatenate([x[:, s]] * (128 // b), axis=0)
        v = jnp.where(r // b == c // b, part, 0.0)
        f = f_ref[s, s]
        size = b
        while size < 128:
            mask = (r // (2 * size) == c // (2 * size)) & (r // size > c // size)
            v = v - dot(v, dot(jnp.where(mask, f, 0.0), v))
            size *= 2
        v_ref[s, s] = v
    size = 128
    while size < W:
        for t in range(0, W, 2 * size):
            lo, hi = slice(t, t + size), slice(t + size, t + 2 * size)
            v_ref[hi, lo] = -dot(v_ref[hi, hi], dot(f_ref[hi, lo], v_ref[lo, lo]))
        size *= 2


def inverse_kernel(f1_ref, f2_ref, v1_ref, v2_ref):
    inverse_of(f1_ref, v1_ref)
    inverse_of(f2_ref, v2_ref)


def inverses(f1, f2):
    shape = jax.ShapeDtypeStruct((W, W), jnp.float32)
    return pl.pallas_call(
        inverse_kernel,
        out_shape=(shape, shape),
        in_specs=[VMEM_SPEC] * 2,
        out_specs=(VMEM_SPEC,) * 2,
        compiler_params=pltpu.CompilerParams(vmem_limit_bytes=32 << 20),
        cost_estimate=pl.CostEstimate(flops=10**10, bytes_accessed=4 << 20, transcendentals=0),
        name="inverses",
    )(f1, f2)


def split(x):
    hi = x.astype(jnp.bfloat16)
    return hi, (x - hi.astype(jnp.float32)).astype(jnp.bfloat16)


def dot_split(left, right, dims=(((1,), (0,)), ((), ()))):
    (a, b), (c, d) = left, right

    def one(x, y):
        return lax.dot_general(x, y, dims, preferred_element_type=jnp.float32)

    return one(a, c) + (one(b, c) + one(a, d))


def dot3(left, right):
    return dot_split(split(left), split(right))


def cross3(left, right):
    return dot_split(split(left), split(right), (((0,), (0,)), ((), ())))


UPPER, LOWER = 72, 64


def accumulate(place, s_ref, acc, offset, pieces):
    xl, z, core = place[0], place[1], place[2]
    at = lax.rem(z + offset + 8, 8) * 128
    first = core == 0
    columns, rows = [], []
    for side in range(2):
        start = pl.multiple_of((xl if side == 0 else 1 - xl) * 1024 + at, 128)
        columns.append(s_ref[:, pl.ds(start, 128)])
    for part in range(2):
        sides = []
        for own, other in pieces:
            span = slice(part * 64, part * 64 + 64)
            sides += [jnp.where(first, own[span], other[span]), jnp.where(first, other[span], own[span])]
        rows.append(jnp.concatenate(sides, axis=0))
    return acc + dot3(jnp.concatenate(columns, axis=1), jnp.concatenate(rows, axis=1))


def both_sides(own_ref, other_ref):
    return [(own_ref[:128, :], other_ref[:128, :]), (own_ref[128:, :], other_ref[128:, :])]


NEAR = (0, -1, 1, -2, 2)


def near_kernel(place_ref, s_ref, *refs):
    found, la_in = refs[:10], refs[10:14]
    acc_ref, la_ref = refs[14:]
    place = [place_ref[i] for i in range(5)]
    for j, offset in enumerate(NEAR):
        pieces = both_sides(found[2 * j], found[2 * j + 1])
        acc_ref[...] = accumulate(place, s_ref, 0.0 if j == 0 else acc_ref[...], offset, pieces)
    for dy in range(4):
        for dx in range(2):
            block = lax.rem(place[3] + dy, 4) * 2 + (place[4] if dx == 0 else 1 - place[4])
            rows = pl.ds(pl.multiple_of(block * 64, 64), 64)
            la_ref[rows, :W] = la_in[dy][dx * 128 : dx * 128 + 64, :]
            la_ref[rows, W:] = la_in[dy][dx * 128 + 64 : dx * 128 + 128, :]


def chunks_of(place):
    y, x = place[3], place[4] * 2 + place[0]
    for ry in range(4):
        for rx in range(4):
            yield ry, rx, lax.rem(y + ry, 4) * 4 + lax.rem(x + rx, 4)


def far_kernel(place_ref, s_ref, acc_ref, la_ref, u1_ref, u2_ref, l1_ref, l2_ref, *refs):
    found = refs[:8]
    p_ref, keep_a, keep_b, send_a, send_b, mixed_ref, a21_ref, diagonal_ref = refs[8:]
    place = [place_ref[i] for i in range(5)]
    acc = acc_ref[...]
    for j, offset in enumerate((-3, 3)):
        acc = accumulate(place, s_ref, acc, offset, both_sides(found[2 * j], found[2 * j + 1]))
    pieces = [(found[4][...], found[5][...]), (found[6][...], found[7][...])]
    p_ref[...] = -2.0 * accumulate(place, s_ref, acc, 4, pieces)
    a22 = cross3(p_ref[:, W:], la_ref[:, W:]) + cross3(u2_ref[...], l2_ref[...])
    a21_ref[...] = cross3(p_ref[:, W:], la_ref[:, :W]) + cross3(u2_ref[...], l1_ref[...])
    a11t = cross3(la_ref[:, :W], p_ref[:, :W]) + cross3(l1_ref[...], u1_ref[...])
    r, c = iota((W, W), 0), iota((W, W), 1)
    mixed_ref[...] = jnp.where(r >= c, a22, a11t)
    diagonal = jnp.sum(jnp.where(r == c, a11t, 0.0), axis=0, keepdims=True)
    diagonal_ref[...] = jnp.concatenate(
        [diagonal[:, t * 128 : (t + 1) * 128] for t in range(4)] + [jnp.zeros((4, 128), jnp.float32)], axis=0
    )

    def write(a_ref, b_ref, source, with_diagonal):
        for ry, rx, chunk in chunks_of(place):
            rows = pl.ds(pl.multiple_of(chunk * 32, 32), 32)
            for t in range(2):
                span = slice(t * 32, (t + 1) * 32)
                a_ref[ry * 4 + rx, span, :] = source[rows, t * 128 : (t + 1) * 128]
                b_ref[rx * 4 + ry, span, :] = source[rows, 256 + t * 128 : 256 + (t + 1) * 128]
            kept = jnp.where(chunk == 0, diagonal_ref[...], 0.0) if with_diagonal else jnp.zeros((8, 128), jnp.float32)
            a_ref[ry * 4 + rx, LOWER:, :] = kept

    @pl.when(place[2] == 0)
    def _():
        write(keep_a, keep_b, mixed_ref, True)
        write(send_a, send_b, a21_ref, False)

    @pl.when(place[2] != 0)
    def _():
        write(keep_a, keep_b, a21_ref, False)
        write(send_a, send_b, mixed_ref, True)


SCRATCH = [pltpu.VMEM((W, W), jnp.float32)] * 2 + [pltpu.VMEM((8, 128), jnp.float32)]


def chol_grad(f, x, v, r, c):
    product = cross3(f, jnp.where(r >= c, x, 0.0))
    halved = jnp.where(r > c, product, jnp.where(r == c, 0.5 * product, 0.0))
    inner = cross3(v, dot3(halved, v))
    return 0.5 * (inner + inner.T)


def tail_kernel(place_ref, *refs):
    mine, theirs = refs[:4], refs[4:8]
    f1_ref, f2_ref, v1_ref, v2_ref, link_ref, adj_ref, out_ref, mixed_ref, a21_ref, diagonal_ref = refs[8:]
    place = [place_ref[i] for i in range(5)]

    def read(ref, source, with_diagonal):
        for ry, rx, chunk in chunks_of(place):
            rows = pl.ds(pl.multiple_of(chunk * 32, 32), 32)
            for t in range(4):
                start = t * 32 + (UPPER - LOWER if t >= 2 else 0)
                ref[rows, t * 128 : (t + 1) * 128] = source[ry][rx, start : start + 32, :]
            if with_diagonal:

                @pl.when(chunk == 0)
                def _():
                    diagonal_ref[...] = source[ry][rx, LOWER:UPPER, :]

    first = place[2] == 0

    @pl.when(first)
    def _():
        read(mixed_ref, mine, True)
        read(a21_ref, theirs, False)

    @pl.when(jnp.logical_not(first))
    def _():
        read(mixed_ref, theirs, True)
        read(a21_ref, mine, False)

    r, c = iota((W, W), 0), iota((W, W), 1)
    diagonal = jnp.concatenate([diagonal_ref[t : t + 1, :] for t in range(4)], axis=1)
    mixed = mixed_ref[...]
    a22 = jnp.where(r >= c, mixed, 0.0)
    a11 = jnp.where(r > c, mixed.T, jnp.where(r == c, diagonal, 0.0))
    link, v1, v2 = link_ref[...], v1_ref[...], v2_ref[...]
    grad_two = chol_grad(f2_ref[...], adj_ref[1] - cross3(v2, a22), v2, r, c)
    out_ref[2] = grad_two
    cross_link = cross3(v2, a21_ref[...])
    cross_one = cross3(v1, a11 - cross3(link, cross_link))
    link_input = dot3(-cross_link - 2.0 * dot3(grad_two, link), v1)
    out_ref[1] = link_input
    out_ref[0] = chol_grad(f1_ref[...], adj_ref[0] - cross3(link_input, link) - cross_one, v1, r, c)


def strips_kernel(_, mine_ref, u1_ref, u2_ref, v1_ref, v2_ref, link_ref, one_ref, two_ref):
    pressed = jnp.sum(mine_ref[...], axis=0)
    two = dot3(u2_ref[...] + pressed[:, W:], v2_ref[...])
    two_ref[...] = two
    one_ref[...] = dot3(u1_ref[...] + pressed[:, :W] - dot3(two, link_ref[...]), v1_ref[...])


def ring(n, d):
    return [(i, (i + d) % n) for i in range(n)]


def x_ring(d):
    moves = []
    for i in range(4):
        x = ((i % 2) * 2 + i // 2 + d) % 4
        moves.append((i, (x % 2) * 2 + x // 2))
    return moves


def swap_cores(x):
    return lax.ppermute(x, "core", SWAP)


def z_step(up, down):
    return lax.ppermute(up, "z", ring(8, 1)), lax.ppermute(down, "z", ring(8, -1))


def paired(found):
    return [x for piece in found for x in (piece, swap_cores(piece))]


def fours(kept, came):
    return [kept[4 * d : 4 * d + 4] + came[4 * d : 4 * d + 4] for d in range(4)]


def along_x(x, d):
    return lax.ppermute(x, ("xl", "xh"), x_ring(d))


def along_y(x, d):
    return lax.ppermute(x, "y", ring(4, d))


def reduce_all(keep_a, keep_b, send_a, send_b):
    a, b = fours(keep_a, swap_cores(send_a)), fours(keep_b, swap_cores(send_b))
    a = a[0] + sum(along_y(a[d], d) for d in (1, 2, 3))
    b = b[0] + sum(along_x(b[d], d) for d in (1, 2, 3))
    a = a[0] + sum(along_x(a[d], d) for d in (1, 2, 3))
    b = b[0] + sum(along_y(b[d], d) for d in (1, 2, 3))
    share = jnp.concatenate([a, b], axis=0)
    reduced = share
    for d in (1, 2, 4):
        reduced = reduced + lax.ppermute(reduced, "z", [(i, i ^ d) for i in range(8)])
    line = jnp.stack([reduced] + [along_x(reduced, -d) for d in (1, 2, 3)])
    ours = [line] + [along_y(line, -d) for d in (1, 2, 3)]
    return share, ours, [swap_cores(piece) for piece in ours]


def local(trail, l1, l2, u1, u2, f1, f2, link, adjoint):
    place = jnp.stack([lax.axis_index(name) for name in AXES])
    matrix = trail.reshape(W, 2048)
    own = jnp.concatenate([l1, l2], axis=0)
    start = jnp.concatenate([own, lax.ppermute(own, "xl", SWAP)], axis=0)
    start, matrix = lax.optimization_barrier((start, matrix))
    up1, down1 = z_step(start, start)
    pair = jnp.concatenate([own, lax.ppermute(own, "xh", SWAP)], axis=0)
    block_row = [pair] + [along_y(pair, -d) for d in (1, 2, 3)]
    up1, down1, v1, v2 = lax.optimization_barrier((up1, down1, *inverses(f1, f2)))
    up2, down2 = z_step(up1, down1)
    up3, down3 = z_step(up2, down2)
    near = paired([start, up1, down1, up2, down2])
    acc, la = call(
        near_kernel, (floats(W, 2 * W),) * 2, (place, matrix, *near, *block_row), flops=4 * 10**9, name="near"
    )
    up3, down3, acc, la = lax.optimization_barrier((up3, down3, acc, la))
    far = paired([up3, down3, *z_step(up3[:128], down3[128:])])
    halves = (floats(16, UPPER, 128), floats(16, LOWER, 128)) * 2
    product, *halves = call(
        far_kernel,
        (floats(W, 2 * W),) + halves,
        (place, matrix, acc, la, u1, u2, l1, l2, *far),
        SCRATCH,
        flops=6 * 10**9,
        name="far",
    )
    share, ours, theirs = reduce_all(*halves)
    product, _ = lax.optimization_barrier((product, share))
    mine = lax.all_to_all(product, COL, 0, 0, tiled=True)
    grads = call(
        tail_kernel,
        floats(3, W, W),
        (place, *ours, *theirs, f1, f2, v1, v2, link, adjoint),
        SCRATCH,
        flops=10**10,
        name="tail",
    )
    strips = call(
        strips_kernel, (floats(64, W),) * 2, (place, mine.reshape(8, 64, 2 * W), u1, u2, v1, v2, link), name="strips"
    )
    return *strips, grads


def solution(mesh):
    fine = Mesh(mesh.devices.reshape(2, 8, 2, 4, 2), AXES)
    strip = P(ROW + COL, None)
    return jax.shard_map(
        local,
        mesh=fine,
        in_specs=(P(ROW, None, COL, None), strip, strip, strip, strip, P(), P(), P(), P()),
        out_specs=(strip, strip, P()),
        check_vma=False,
    )
```

```python
import jax
import jax.numpy as jnp
from jax import lax
from jax.experimental import pallas as pl
from jax.experimental.pallas import tpu as pltpu
from jax.sharding import Mesh, PartitionSpec as P

AXES = ("xl", "z", "core", "y", "xh")
ROW = ("xl", "z", "core")
COL = ("y", "xh")
PLANE = ("y", "xh", "xl")
HIGHEST = lax.Precision.HIGHEST
HIGH = lax.Precision.HIGH
SWAP = [(0, 1), (1, 0)]
W = 512
BASE = 16
SMEM_SPEC = pl.BlockSpec(memory_space=pltpu.SMEM)
ANY_SPEC = pl.BlockSpec(memory_space=pl.ANY)


def whole(x):
    return pl.BlockSpec(x.shape, lambda _: (0,) * len(x.shape), pipeline_mode=pl.Buffered(1))


def call(kernel, outs, operands, scratch=(), flops=10**9, name=None, fetched=0, placed=0):
    kept = len(operands) - fetched
    specs = [whole(x) for x in outs]
    return pl.pallas_call(
        kernel,
        grid=(1,),
        out_shape=outs,
        in_specs=[SMEM_SPEC] + [whole(x) for x in operands[1:kept]] + [ANY_SPEC] * fetched,
        out_specs=[ANY_SPEC] * placed + specs[placed:],
        scratch_shapes=list(scratch),
        compiler_params=pltpu.CompilerParams(vmem_limit_bytes=62 << 20),
        cost_estimate=pl.CostEstimate(flops=flops, bytes_accessed=16 << 20, transcendentals=0),
        name=name,
    )(*operands)


def floats(*shape):
    return jax.ShapeDtypeStruct(shape, jnp.float32)


def dot(left, right, precision=HIGHEST):
    return jnp.dot(left, right, precision=precision, preferred_element_type=jnp.float32)


def cross(left, right, precision=HIGHEST):
    return lax.dot_general(
        left, right, (((0,), (0,)), ((), ())), precision=precision, preferred_element_type=jnp.float32
    )


def iota(shape, dim):
    return lax.broadcasted_iota(jnp.int32, shape, dim)


def inverse_of(f_ref, v_ref):
    b = BASE
    lane = iota((b, W), 1)
    row = iota((b, W), 0)
    diag = jnp.zeros((b, W), jnp.float32)
    for k in range(W // b):
        diag = jnp.where(lane // b == k, f_ref[k * b : (k + 1) * b, :], diag)
    spread = (iota((128, 128), 0) // b == iota((128, 128), 1) // b).astype(jnp.float32)
    columns = []
    for t in range(W // 128):
        part = diag[:, t * 128 : (t + 1) * 128]
        inner = iota((b, 128), 1) % b
        stack = jnp.concatenate([jnp.where(inner == k, part, 0.0) for k in range(b)], axis=0)
        columns.append(dot(stack, spread))
    spread_f = jnp.concatenate(columns, axis=1)
    x = (lane % b == row).astype(jnp.float32)
    for k in range(b):
        f_k = spread_f[k * b : (k + 1) * b, :]
        x_k = x[k : k + 1, :] / f_k[k : k + 1, :]
        x = jnp.where(row == k, x_k, jnp.where(row > k, x - f_k * x_k, x))
    v_ref[...] = jnp.zeros((W, W), jnp.float32)
    r, c = iota((128, 128), 0), iota((128, 128), 1)
    for t in range(W // 128):
        s = slice(t * 128, (t + 1) * 128)
        part = jnp.concatenate([x[:, s]] * (128 // b), axis=0)
        v = jnp.where(r // b == c // b, part, 0.0)
        f = f_ref[s, s]
        size = b
        while size < 128:
            mask = (r // (2 * size) == c // (2 * size)) & (r // size > c // size)
            v = v - dot(v, dot(jnp.where(mask, f, 0.0), v))
            size *= 2
        v_ref[s, s] = v
    size = 128
    while size < W:
        for t in range(0, W, 2 * size):
            lo, hi = slice(t, t + size), slice(t + size, t + 2 * size)
            v_ref[hi, lo] = -dot(v_ref[hi, hi], dot(f_ref[hi, lo], v_ref[lo, lo]))
        size *= 2


def pack(ref, at, x):
    ref[at], ref[at + 1] = split(x)


def inverse_kernel(_, f_ref, link_ref, v_ref, pack_ref):
    inverse_of(f_ref, v_ref)
    pack(pack_ref, 0, v_ref[...].T)
    pack(pack_ref, 2, v_ref[...])
    pack(pack_ref, 4, f_ref[...].T)
    pack(pack_ref, 6, link_ref[...])


def split(x):
    hi = x.astype(jnp.bfloat16)
    return hi, (x - hi.astype(jnp.float32)).astype(jnp.bfloat16)


def dot_split(left, right, dims=(((1,), (0,)), ((), ()))):
    (a, b), (c, d) = left, right

    def one(x, y):
        return lax.dot_general(x, y, dims, preferred_element_type=jnp.float32)

    return one(a, c) + (one(b, c) + one(a, d))


def dot3(left, right):
    return dot_split(split(left), split(right))


def cross3(left, right):
    return dot_split(split(left), split(right), (((0,), (0,)), ((), ())))


def columns_at(place, offset):
    at = lax.rem(place[1] + offset + 8, 8) * 128
    return [pl.multiple_of(side * 1024 + at, 128) for side in (place[0], 1 - place[0])]


def accumulate(place, columns, pieces):
    first = place[2] == 0
    rows = []
    for part in range(2):
        sides = []
        for own, other in pieces:
            span = slice(part * 64, part * 64 + 64)
            sides += [jnp.where(first, own[span], other[span]), jnp.where(first, other[span], own[span])]
        rows.append(jnp.concatenate(sides, axis=0))
    return dot3(columns, jnp.concatenate(rows, axis=1))


def both_sides(own_ref, other_ref):
    return [(own_ref[:128, :], other_ref[:128, :]), (own_ref[128:, :], other_ref[128:, :])]


NEAR = (0, -1, 1, -2, 2)


def near_kernel(place_ref, s_ref, *refs):
    found, la_in = refs[:10], refs[10:14]
    acc_ref, la_ref = refs[14:]
    place = [place_ref[i] for i in range(5)]
    for j, offset in enumerate(NEAR):
        pieces = both_sides(found[2 * j], found[2 * j + 1])
        columns = jnp.concatenate([s_ref[:, pl.ds(start, 128)] for start in columns_at(place, offset)], axis=1)
        part = accumulate(place, columns, pieces)
        acc_ref[...] = part if j == 0 else acc_ref[...] + part
    for dy in range(4):
        for dx in range(2):
            block = lax.rem(place[3] + dy, 4) * 2 + (place[4] if dx == 0 else 1 - place[4])
            rows = pl.ds(pl.multiple_of(block * 64, 64), 64)
            la_ref[rows, :W] = la_in[dy][dx * 128 : dx * 128 + 64, :]
            la_ref[rows, W:] = la_in[dy][dx * 128 + 64 : dx * 128 + 128, :]


def chunks_of(place):
    for chunk in range(16):
        yield chunk, slice(chunk * 32, (chunk + 1) * 32)


def far_kernel(place_ref, s_hbm, acc_hbm, *refs):
    found_hbm, (la_hbm, u1_hbm, u2_hbm, l1_hbm, l2_hbm) = refs[:8], refs[8:13]
    p_hbm, keep_ref, send_ref = refs[13:16]
    s_ref, p_ref, la_ref, u1_ref, u2_ref, l1_ref, l2_ref = refs[16:23]
    found, sem = refs[23:31], refs[31]
    place = [place_ref[i] for i in range(5)]
    offsets = (-3, 3, 4)
    pairs = []
    for j, offset in enumerate(offsets):
        for side, start in enumerate(columns_at(place, offset)):
            at = (2 * j + side) * 128
            pairs.append((s_hbm.at[:, pl.ds(start, 128)], s_ref.at[:, at : at + 128]))
    pairs += list(zip(found_hbm, found))
    pairs += [(acc_hbm, p_ref), (la_hbm, la_ref)]
    pairs += [(u1_hbm, u1_ref), (u2_hbm, u2_ref), (l1_hbm, l1_ref), (l2_hbm, l2_ref)]
    copies = [pltpu.make_async_copy(a, b, sem.at[i]) for i, (a, b) in enumerate(pairs)]
    for copy in copies:
        copy.start()

    def arrive(first, last):
        for copy in copies[first:last]:
            copy.wait()

    arrive(0, 14)
    total = accumulate(place, s_ref[:, :256], both_sides(found[0], found[1]))
    total += accumulate(place, s_ref[:, 256:512], both_sides(found[2], found[3]))
    pieces = [(found[4][...], found[5][...]), (found[6][...], found[7][...])]
    total += accumulate(place, s_ref[:, 512:], pieces)
    arrive(14, 15)
    p_ref[...] = -2.0 * (p_ref[...] + total)
    out = pltpu.make_async_copy(p_ref, p_hbm, sem.at[20])
    out.start()
    arrive(15, 20)
    panels = jnp.concatenate([l1_ref[...], l2_ref[...]], axis=1)
    with_two = cross3(p_ref[:, W:], la_ref[...]) + cross3(u2_ref[...], panels)
    a11t = cross3(la_ref[:, :W], p_ref[:, :W]) + cross3(l1_ref[...], u1_ref[...])
    r, c = iota((W, W), 0), iota((W, W), 1)
    a21 = with_two[:, :W]
    mixed = jnp.where(r >= c, with_two[:, W:], a11t)
    diagonal = jnp.sum(jnp.where(r == c, a11t, 0.0), axis=0, keepdims=True)

    def write(ref, x):
        for chunk, rows in chunks_of(place):
            for t in range(4):
                ref[chunk, t * 32 : (t + 1) * 32, :] = x[rows, t * 128 : (t + 1) * 128]
        ref[:, 128:, :] = jnp.zeros((16, 8, 128), jnp.float32)

    def write_diagonal(ref):
        for t in range(4):
            ref[0, 128 + t : 129 + t, :] = diagonal[:, t * 128 : (t + 1) * 128]

    @pl.when(place[2] == 0)
    def _():
        write(keep_ref, mixed)
        write_diagonal(keep_ref)
        write(send_ref, a21)

    @pl.when(place[2] != 0)
    def _():
        write(keep_ref, a21)
        write(send_ref, mixed)
        write_diagonal(send_ref)

    out.wait()


def vmem(*shape):
    return pltpu.VMEM(shape, jnp.float32)


FAR_SCRATCH = (
    [vmem(W, 768), vmem(W, 2 * W), vmem(W, 2 * W)]
    + [vmem(64, W)] * 4
    + [vmem(256, W)] * 4
    + [vmem(128, W)] * 4
    + [pltpu.SemaphoreType.DMA((21,))]
)
TAIL_SCRATCH = (
    [vmem(W, W)] * 2
    + [vmem(8, 128), vmem(3, W, W), vmem(2, W, W)]
    + [pltpu.VMEM((8, W, W), jnp.bfloat16)] * 2
    + [pltpu.SemaphoreType.DMA((6,))]
)


def pair_at(ref, at):
    return ref[at], ref[at + 1]


H = W // 2
TOP, LOW = slice(0, H), slice(H, W)
ALL = slice(0, W)


def at(pair, rows, columns):
    return pair[0][rows, columns], pair[1][rows, columns]


def beside(left, right):
    return jnp.concatenate([left, right], axis=1)


def above(top, bottom):
    return jnp.concatenate([top, bottom], axis=0)


def zeros():
    return jnp.zeros((H, H), jnp.float32)


def upper_any(u, x):
    return above(dot_split(at(u, TOP, ALL), x), dot_split(at(u, LOW, LOW), at(x, LOW, ALL)))


def upper_lower(u, x, whole_result):
    corner = dot_split(at(u, TOP, LOW), at(x, LOW, LOW)) if whole_result else zeros()
    top = beside(dot_split(at(u, TOP, ALL), at(x, ALL, TOP)), corner)
    return above(top, dot_split(at(u, LOW, LOW), at(x, LOW, ALL)))


def lower_lower(x, y):
    top = beside(dot_split(at(x, TOP, TOP), at(y, TOP, TOP)), zeros())
    bottom = beside(dot_split(at(x, LOW, ALL), at(y, ALL, TOP)), dot_split(at(x, LOW, LOW), at(y, LOW, LOW)))
    return above(top, bottom)


def any_lower(x, y):
    return beside(dot_split(x, at(y, ALL, TOP)), dot_split(at(x, ALL, LOW), at(y, LOW, LOW)))


def lower_part(x, y):
    top = beside(dot_split(at(x, TOP, ALL), at(y, ALL, TOP)), zeros())
    return above(top, dot_split(at(x, LOW, ALL), y))


def chol_grad(pack_ref, x, r, c):
    product = upper_lower(pair_at(pack_ref, 4), split(jnp.where(r >= c, x, 0.0)), False)
    halved = jnp.where(r > c, product, jnp.where(r == c, 0.5 * product, 0.0))
    inner = lower_lower(split(halved), pair_at(pack_ref, 2))
    inner = upper_lower(pair_at(pack_ref, 0), split(inner), True)
    return 0.5 * (inner + inner.T)


def tail_kernel(place_ref, *refs):
    ours, theirs, (two_hbm, adj_hbm, one_hbm, out_hbm) = refs[:4], refs[4:8], refs[8:12]
    mixed_ref, a21_ref, diagonal_ref, out_ref, adj_ref, two_ref, one_ref, sem = refs[12:]
    pairs = ((two_hbm, two_ref), (adj_hbm, adj_ref), (one_hbm, one_ref))
    copies = [pltpu.make_async_copy(a, b, sem.at[i]) for i, (a, b) in enumerate(pairs)]
    for copy in copies:
        copy.start()
    place = [place_ref[i] for i in range(5)]

    y, x = place[3], place[4] * 2 + place[0]

    def read(ref, source):
        for ry in range(4):
            for rx in range(4):
                chunk = lax.rem(y + ry, 4) * 4 + lax.rem(x + rx, 4)
                rows = pl.ds(pl.multiple_of(chunk * 32, 32), 32)
                for t in range(4):
                    ref[rows, t * 128 : (t + 1) * 128] = source[ry][rx, t * 32 : (t + 1) * 32, :]

    def read_diagonal(source):
        diagonal_ref[...] = sum(source[ry][rx, 128:, :] for ry in range(4) for rx in range(4))

    first = place[2] == 0

    @pl.when(first)
    def _():
        read(mixed_ref, ours)
        read_diagonal(ours)
        read(a21_ref, theirs)

    @pl.when(jnp.logical_not(first))
    def _():
        read(mixed_ref, theirs)
        read_diagonal(theirs)
        read(a21_ref, ours)

    outs = [pltpu.make_async_copy(out_ref.at[i], out_hbm.at[i], sem.at[3 + i]) for i in range(3)]
    r, c = iota((W, W), 0), iota((W, W), 1)
    diagonal = jnp.concatenate([diagonal_ref[t : t + 1, :] for t in range(4)], axis=1)
    mixed = mixed_ref[...]
    a22 = jnp.where(r >= c, mixed, 0.0)
    a11 = jnp.where(r > c, mixed.T, jnp.where(r == c, diagonal, 0.0))
    copies[0].wait()
    copies[1].wait()
    cross_two = upper_lower(pair_at(two_ref, 0), split(a22), False)
    cross_link = upper_any(pair_at(two_ref, 0), split(a21_ref[...]))
    grad_two = chol_grad(two_ref, adj_ref[1] - cross_two, r, c)
    out_ref[2] = grad_two
    outs[2].start()
    copies[2].wait()
    link, turned_link = pair_at(two_ref, 6), pair_at(one_ref, 6)
    link_input = any_lower(split(-cross_link - 2.0 * dot_split(split(grad_two), link)), pair_at(one_ref, 2))
    out_ref[1] = link_input
    outs[1].start()
    rest = jnp.where(r >= c, a11 - lower_part(turned_link, split(cross_link)), 0.0)
    cross_one = upper_lower(pair_at(one_ref, 0), split(rest), False)
    linked = lower_part(split(link_input.T), link)
    out_ref[0] = chol_grad(one_ref, adj_ref[0] - linked - cross_one, r, c)
    outs[0].start()
    for copy in outs:
        copy.wait()


def strips_kernel(_, mine_ref, u1_ref, u2_ref, v1_ref, v2_ref, link_ref, one_ref, two_ref):
    pressed = jnp.sum(mine_ref[...], axis=0)
    two = dot3(u2_ref[...] + pressed[:, W:], v2_ref[...])
    two_ref[...] = two
    one_ref[...] = dot3(u1_ref[...] + pressed[:, :W] - dot3(two, link_ref[...]), v1_ref[...])


def ring(n, d):
    return [(i, (i + d) % n) for i in range(n)]


def x_ring(d):
    moves = []
    for i in range(4):
        x = ((i % 2) * 2 + i // 2 + d) % 4
        moves.append((i, (x % 2) * 2 + x // 2))
    return moves


def swap_cores(x):
    return lax.ppermute(x, "core", SWAP)


def z_step(up, down):
    return lax.ppermute(up, "z", ring(8, 1)), lax.ppermute(down, "z", ring(8, -1))


def paired(found):
    return [x for piece in found for x in (piece, swap_cores(piece))]


def along_y(x, d):
    return lax.ppermute(x, "y", ring(4, d))


def reduce_plane(keep, send):
    half = keep + swap_cores(send)
    return jnp.sum(lax.all_to_all(half, PLANE, 0, 0, tiled=True), axis=0)


def reduce_z(share):
    came = [lax.ppermute(share, "z", [(i, i ^ d) for i in range(8)]) for d in (1, 2, 3)]
    share = share + came[0] + (came[1] + came[2])
    return share + lax.ppermute(share, "z", [(i, i ^ 4) for i in range(8)])


def along_x(x, d):
    return lax.ppermute(x, ("xl", "xh"), x_ring(d))


def gather_plane(share, strips):
    line = jnp.stack([share] + [along_x(share, -d) for d in (1, 2, 3)])
    came, strips = lax.optimization_barrier(([along_y(line, -d) for d in (1, 2, 3)], strips))
    ours = [line] + came
    return ours, [swap_cores(piece) for piece in ours], strips


def local(trail, l1, l2, u1, u2, f1, f2, link, adjoint):
    place = jnp.stack([lax.axis_index(name) for name in AXES])
    matrix = trail.reshape(W, 2048)
    own = jnp.concatenate([l1, l2], axis=0)
    start = jnp.concatenate([own, lax.ppermute(own, "xl", SWAP)], axis=0)
    pair = jnp.concatenate([own, lax.ppermute(own, "xh", SWAP)], axis=0)
    start, pair, matrix = lax.optimization_barrier((start, pair, matrix))
    up1, down1 = z_step(start, start)
    block_row = [pair] + [along_y(pair, -d) for d in (1, 2, 3)]
    packs = (floats(W, W), jax.ShapeDtypeStruct((8, W, W), jnp.bfloat16))
    v2, pack2 = call(inverse_kernel, packs, (place, f2, link), flops=5 * 10**9, name="inverse_two")
    up1, down1, v2, pack2 = lax.optimization_barrier((up1, down1, v2, pack2))
    up2, down2 = z_step(up1, down1)
    up3, down3 = z_step(up2, down2)
    near = paired([start, up1, down1, up2, down2])
    acc, la = call(
        near_kernel, (floats(W, 2 * W),) * 2, (place, matrix, *near, *block_row), flops=4 * 10**9, name="near"
    )
    up3, down3, acc, la = lax.optimization_barrier((up3, down3, acc, la))
    far = paired([up3, down3, *z_step(up3[:128], down3[128:])])
    half = floats(16, 136, 128)
    product, keep, send = call(
        far_kernel,
        (floats(W, 2 * W), half, half),
        (place, matrix, acc, *far, la, u1, u2, l1, l2),
        FAR_SCRATCH,
        flops=6 * 10**9,
        name="far",
        fetched=15,
        placed=1,
    )
    share = reduce_plane(keep, send)
    share, product, f1 = lax.optimization_barrier((share, product, f1))
    mine = lax.all_to_all(product, COL, 0, 0, tiled=True)
    v1, pack1 = call(inverse_kernel, packs, (place, f1, link.T), flops=5 * 10**9, name="inverse_one")
    reduced, v1, pack1 = lax.optimization_barrier((reduce_z(share), v1, pack1))
    strips = call(
        strips_kernel, (floats(64, W),) * 2, (place, mine.reshape(8, 64, 2 * W), u1, u2, v1, v2, link), name="strips"
    )
    ours, theirs, strips = gather_plane(reduced, strips)
    (grads,) = call(
        tail_kernel,
        (floats(3, W, W),),
        (place, *ours, *theirs, pack2, adjoint, pack1),
        TAIL_SCRATCH,
        flops=10**10,
        name="tail",
        fetched=3,
        placed=1,
    )
    return *strips, grads


def solution(mesh):
    fine = Mesh(mesh.devices.reshape(2, 8, 2, 4, 2), AXES)
    strip = P(ROW + COL, None)
    return jax.shard_map(
        local,
        mesh=fine,
        in_specs=(P(ROW, None, COL, None), strip, strip, strip, strip, P(), P(), P(), P()),
        out_specs=(strip, strip, P()),
        check_vma=False,
    )
```
